32 devices in a mesh: ctx: 8 (over z, core), head: 4 (over y, x).
Axes of the slice: x: 2, y: 2, z: 4, core: 2. Of those that a mesh axis runs over, the one named last changes fastest.
Arguments:
- queries: bfloat16 [3072, 32, 128], P(('ctx', 'head')), may hold values from -52 to 52
- key_vectors: bfloat16 [3072, 32, 128], P(('ctx', 'head')), may hold values from -4 to 4
- values: bfloat16 [3072, 32, 128], P(('ctx', 'head')), may hold values from -6 to 6
- directions: bfloat16 [3072, 32, 128], P(('ctx', 'head')), may hold values from -6 to 6
- beta_logit: bfloat16 [3072, 32], P(('ctx', 'head')), may hold values from -4.5 to 9
Outputs:
- attended: bfloat16 [3072, 32, 128], P(('ctx', 'head'))
The draws below stay inside these ranges and needn't reach their ends.
All inputs are finite; a program needn't handle non-finite values.
Results may differ from the reference program's by a relative error of at most 0.0052.
Values may be sent and summed in bfloat16 or wider, within the bound.
A program may use at most 64 MiB of HBM per device.

```python
import jax
import jax.numpy as jnp
from jax import lax

HEADS = 32
HEAD_DIM = 128
SUB = 64
TOK_BLK = 384
TOKEN_TOTAL = 3072


def queries_and_keys(key):
    shape = (TOKEN_TOTAL, HEADS, HEAD_DIM)
    base_keys = jax.random.fold_in(key, 11)
    base_queries = jax.random.fold_in(key, 12)
    key_rows = jnp.clip(jax.random.normal(base_keys, shape, jnp.float32), -4.0, 4.0)
    query_rows = jnp.clip(jax.random.normal(base_queries, shape, jnp.float32), -4.0, 4.0)
    return (query_rows, key_rows)


def draw_queries(key, part):
    return queries_and_keys(key)[0].astype(jnp.bfloat16)


def draw_key_vectors(key, part):
    return queries_and_keys(key)[1].astype(jnp.bfloat16)


def draw_beta_logit(key, part):
    shape = (TOKEN_TOTAL, HEADS)
    reach = jnp.log(jnp.maximum(2.0 * TOKEN_TOTAL / HEAD_DIM, 2.0))
    slow_heads = jax.random.randint(jax.random.fold_in(key, 21), (HEADS,), 0, 2) == 1
    steady = reach + 0.5 + 2.0 * jax.random.uniform(jax.random.fold_in(key, 22), shape, jnp.float32)
    quick = jnp.clip(1.5 * jax.random.normal(jax.random.fold_in(key, 23), shape, jnp.float32), -4.5, 4.5)
    score_logits = jnp.where(slow_heads[None, :], steady, quick)
    sequence_spans = jax.random.randint(jax.random.fold_in(key, 24), (TOKEN_TOTAL, 1), 0, 512) == 0
    score_logits = jnp.where(sequence_spans, 0.0, score_logits)
    return score_logits.astype(jnp.bfloat16)


def level_of(stream_key, shape, cuts, least, top_value):
    def one(axis_at, parts):
        draws = jax.random.uniform(jax.random.fold_in(jax.random.fold_in(stream_key, 6), axis_at), (parts,), jnp.float32, least / len(cuts), top_value / len(cuts))
        return jnp.repeat(jnp.exp(draws), shape[axis_at] // parts).reshape((-1,) + (1,) * (len(shape) - axis_at - 1))

    loudness = one(*cuts[0])
    for cut in cuts[1:]:
        loudness = loudness * one(*cut)
    return loudness


def gaussian(own_key, dims, scale, most, cuts=(), kind=jnp.bfloat16):
    drawn = jax.random.normal(own_key, dims, jnp.float32) * scale
    if len(cuts) > 0:
        drawn = level_of(own_key, dims, cuts, -0.22, 0.18) * drawn
    return jnp.clip(drawn, min=-most, max=most).astype(kind)


def setup_inputs(seed: int = 0) -> dict:
    splits = jax.random.split(jax.random.key(seed), 6)
    queries = draw_queries(jax.random.fold_in(splits[5], 71), 0)
    key_vectors = draw_key_vectors(jax.random.fold_in(splits[5], 71), 0)
    values = gaussian(splits[2], (TOKEN_TOTAL, HEADS, HEAD_DIM), 1.0, 6.0, ((0, 32),))
    directions = gaussian(splits[3], (TOKEN_TOTAL, HEADS, HEAD_DIM), 1.0, 6.0, ((0, 32),))
    beta_logit = draw_beta_logit(jax.random.fold_in(splits[5], 71), 0)
    return dict(queries=queries, key_vectors=key_vectors, values=values, directions=directions, beta_logit=beta_logit)


precise = lax.Precision.HIGHEST
far_below = -1e+30

def round_half(array):
    return lax.optimization_barrier(array.astype(jnp.bfloat16)).astype(jnp.float32)

def widen(array):
    return array.astype(jnp.float32)

def unit_rows(directions):
    widened = directions.astype(jnp.float32)
    return widened * lax.rsqrt(lax.optimization_barrier(jnp.sum(widened * widened, axis=-1, keepdims=True)) + 1e-06)

def sub_blocks(query_float, key_float, unit_dirs, beta_rate, sub_size):
    row_count, head_count, head_width = query_float.shape
    sub_count = row_count // sub_size
    query_sub = query_float.reshape(sub_count, sub_size, head_count, head_width)
    key_sub = key_float.reshape(sub_count, sub_size, head_count, head_width)
    dir_sub = unit_dirs.reshape(sub_count, sub_size, head_count, head_width)
    rate_sub = beta_rate.reshape(sub_count, sub_size, head_count)
    positions = lax.iota(jnp.int32, sub_size)
    strictly_lower = positions[:, None] > positions[None, :]
    lower_incl = positions[:, None] >= positions[None, :]
    identity_sub = jnp.eye(sub_size, dtype=jnp.float32)
    gram_matrix = jnp.einsum('nahe,nbhe->nhab', dir_sub, dir_sub, precision=precise)
    inv_rate = jnp.transpose(1.0 / rate_sub, (0, 2, 1))
    triangle = jnp.where(strictly_lower, gram_matrix, 0.0) + identity_sub * inv_rate[..., None]
    inverse = jax.scipy.linalg.solve_triangular(triangle, jnp.broadcast_to(identity_sub, triangle.shape), lower=True)
    query_dots = jnp.where(lower_incl, jnp.einsum('nihe,nahe->nhia', query_sub, dir_sub, precision=precise), 0.0)
    key_dots = jnp.where(strictly_lower.T, jnp.einsum('njhe,nbhe->nhjb', key_sub, dir_sub, precision=precise), 0.0)
    query_mix = jnp.einsum('nhia,nhab->nhib', query_dots, inverse, precision=precise)
    key_mix = jnp.einsum('nhjb,nhab->nhja', key_dots, inverse, precision=precise)
    inner_scores = jnp.einsum('nihe,njhe->nhij', query_sub, key_sub, precision=precise) - jnp.einsum('nhib,nhjb->nhij', query_mix, key_dots, precision=precise)
    start_query = query_sub - jnp.einsum('nhib,nbhe->nihe', query_mix, dir_sub, precision=precise)
    end_keys = key_sub - jnp.einsum('nhja,nahe->njhe', key_mix, dir_sub, precision=precise)
    transport = jnp.eye(head_width, dtype=jnp.float32) - jnp.einsum('nahe,nhab,nbhf->nhef', dir_sub, inverse, dir_sub, precision=precise)
    return (inner_scores, start_query, end_keys, transport)

def frames(inner_scores, start_query, end_keys, transport, sub_size, score_scale):
    sub_count, _, head_count, head_width = start_query.shape
    frame_count = sub_count // 2
    frame_size = 2 * sub_size
    inner_pairs = inner_scores.reshape(frame_count, 2, head_count, sub_size, sub_size)
    query_pairs = start_query.reshape(frame_count, 2, sub_size, head_count, head_width)
    key_pairs = end_keys.reshape(frame_count, 2, sub_size, head_count, head_width)
    map_pairs = transport.reshape(frame_count, 2, head_count, head_width, head_width)
    first_map = map_pairs[:, 0]
    second_map = map_pairs[:, 1]
    lifted_query = jnp.einsum('fihe,fhek->fihk', query_pairs[:, 1], first_map, precision=precise)
    pushed_keys = jnp.einsum('fjhk,fhek->fjhe', key_pairs[:, 0], second_map, precision=precise)
    framed_query_rows = jnp.concatenate([query_pairs[:, 0], lifted_query], axis=1)
    frame_keys = jnp.concatenate([pushed_keys, key_pairs[:, 1]], axis=1)
    frame_map = jnp.einsum('fhek,fhkg->fheg', second_map, first_map, precision=precise)
    cross_scores = jnp.einsum('fihe,fjhe->fhij', query_pairs[:, 1], key_pairs[:, 0], precision=precise)
    blocked = jnp.zeros_like(cross_scores)
    upper_half = jnp.concatenate([inner_pairs[:, 0], blocked], axis=-1)
    lower_half = jnp.concatenate([cross_scores, inner_pairs[:, 1]], axis=-1)
    combined_parts = jnp.concatenate([upper_half, lower_half], axis=2) * score_scale
    positions = lax.iota(jnp.int32, frame_size)
    combined_parts = jnp.where(positions[:, None] >= positions[None, :], combined_parts, far_below)
    return (combined_parts, framed_query_rows, frame_keys, frame_map)

def start_state(combined_parts, frame_values):
    frame_count, head_count, frame_size, _ = combined_parts.shape
    row_maximum = lax.optimization_barrier(jnp.max(combined_parts, axis=-1))
    weights = jnp.exp(combined_parts - row_maximum[..., None])
    row_total = lax.optimization_barrier(jnp.sum(weights, axis=-1))
    weighted = jnp.einsum('fhij,fjhe->fihe', round_half(weights), widen(frame_values), precision=precise)
    row_count = frame_count * frame_size
    row_maximum = jnp.transpose(row_maximum, (0, 2, 1)).reshape(row_count, head_count)
    row_total = jnp.transpose(row_total, (0, 2, 1)).reshape(row_count, head_count)
    weighted = weighted.reshape(row_count, head_count, weighted.shape[-1])
    return (row_maximum, row_total, weighted)

def absorb(softmax_state, scores, value_entries):
    row_maximum, row_total, weighted = softmax_state
    new_max = jnp.maximum(row_maximum, lax.optimization_barrier(jnp.max(scores, axis=-1)))
    factor = jnp.exp(row_maximum - new_max)
    weights = jnp.exp(scores - new_max[..., None])
    row_total = row_total * factor + lax.optimization_barrier(jnp.sum(weights, axis=-1))
    weighted = weighted * factor[..., None] + jnp.einsum('ihj,jhe->ihe', round_half(weights), widen(value_entries), precision=precise)
    return (new_max, row_total, weighted)

def local_block(queries, key_vectors, values, directions, beta_logit, sub_size):
    row_count, head_count, head_width = queries.shape
    score_scale = head_width ** (-0.5)
    unit_dirs = unit_rows(directions)
    beta_rate = 2.0 / (1.0 + jnp.exp(-beta_logit.astype(jnp.float32)))
    inner_scores, start_query, end_keys, transport = sub_blocks(widen(queries), widen(key_vectors), unit_dirs, beta_rate, sub_size)
    combined_parts, framed_query_rows, frame_keys, frame_map = frames(inner_scores, start_query, end_keys, transport, sub_size, score_scale)
    frame_count = combined_parts.shape[0]
    frame_size = 2 * sub_size
    frame_values = values.reshape(frame_count, frame_size, head_count, head_width)
    softmax_state = start_state(combined_parts, frame_values)
    frame_half = round_half(frame_keys)
    frame_of_row = lax.iota(jnp.int32, row_count) // frame_size
    identity_heads = jnp.broadcast_to(jnp.eye(head_width, dtype=jnp.float32), (head_count, head_width, head_width))

    def descend(running, block_index):
        current, softmax_state = running
        is_later = (frame_of_row > block_index)[:, None, None]
        scores = jnp.einsum('ihe,jhe->ihj', round_half(current), frame_half[block_index], precision=precise) * score_scale
        scores = jnp.where(is_later, scores, far_below)
        softmax_state = absorb(softmax_state, scores, frame_values[block_index])
        advanced = jnp.einsum('ihe,hek->ihk', current, frame_map[block_index], precision=precise)
        return ((jnp.where(is_later, advanced, current), softmax_state), None)
    (block_query, softmax_state), _ = lax.scan(descend, (framed_query_rows.reshape(row_count, head_count, head_width), softmax_state), jnp.arange(frame_count - 1, -1, -1, dtype=jnp.int32))

    def ascend(running, block_index):
        current, product = running
        is_earlier = (frame_of_row < block_index)[:, None, None]
        advanced = jnp.einsum('jhk,hek->jhe', current, frame_map[block_index], precision=precise)
        product = jnp.einsum('hek,hkg->heg', frame_map[block_index], product, precision=precise)
        return ((jnp.where(is_earlier, advanced, current), product), None)
    (block_keys, block_map), _ = lax.scan(ascend, (frame_keys.reshape(row_count, head_count, head_width), identity_heads), jnp.arange(frame_count, dtype=jnp.int32))
    return (softmax_state, block_query, block_keys.astype(jnp.bfloat16), block_map)

def remote_absorb(softmax_state, block_query, carried_map, key_half, value_entries, score_scale):
    moved_query = round_half(jnp.einsum('ihe,hek->ihk', block_query, carried_map, precision=precise))
    scores = jnp.einsum('ihe,jhe->ihj', moved_query, widen(key_half), precision=precise) * score_scale
    return absorb(softmax_state, scores, value_entries)

def reference(queries, key_vectors, values, directions, beta_logit):
    token_count, head_count, head_width = queries.shape
    block_count = token_count // TOK_BLK
    score_scale = head_width ** (-0.5)
    identity_one = jnp.eye(head_width, dtype=jnp.float32)[None]

    def per_head(arrays):
        head_query, head_keys, head_values, head_dirs, head_logit = arrays
        shaped = (head_query.reshape(block_count, TOK_BLK, 1, head_width), head_keys.reshape(block_count, TOK_BLK, 1, head_width), head_values.reshape(block_count, TOK_BLK, 1, head_width), head_dirs.reshape(block_count, TOK_BLK, 1, head_width), head_logit.reshape(block_count, TOK_BLK, 1))

        def one_block(pieces):
            return local_block(pieces[0], pieces[1], pieces[2], pieces[3], pieces[4], SUB)
        states, block_query, block_keys, block_map = lax.map(one_block, shaped)
        value_blocks = shaped[2]
        outputs = []
        for query_block in range(block_count):
            softmax_state = jax.tree.map(lambda leaf_array: leaf_array[query_block], states)
            if query_block > 0:
                own_query = block_query[query_block]

                def step_back(running, block_index):
                    inner_state, product = running
                    inner_state = remote_absorb(inner_state, own_query, product, block_keys[block_index], value_blocks[block_index], score_scale)
                    product = jnp.einsum('hek,hkg->heg', product, block_map[block_index], precision=precise)
                    return ((inner_state, product), None)
                (softmax_state, _), _ = lax.scan(step_back, (softmax_state, identity_one), jnp.arange(query_block - 1, -1, -1, dtype=jnp.int32))
            row_maximum, row_total, weighted = softmax_state
            outputs.append(weighted / row_total[..., None])
        return jnp.concatenate(outputs, axis=0)
    stacked = (jnp.moveaxis(queries, 1, 0)[:, :, None, :], jnp.moveaxis(key_vectors, 1, 0)[:, :, None, :], jnp.moveaxis(values, 1, 0)[:, :, None, :], jnp.moveaxis(directions, 1, 0)[:, :, None, :], jnp.moveaxis(beta_logit, 1, 0)[:, :, None])
    result = lax.map(per_head, stacked)
    return jnp.moveaxis(result[:, :, 0, :], 0, 1).astype(jnp.bfloat16)
```

```python
import functools

import jax
import jax.numpy as jnp
from jax import lax
from jax.experimental import pallas as pl
from jax.experimental.pallas import tpu as pltpu
from jax.sharding import PartitionSpec as P

SUB = 64
f32 = jnp.float32
bf16 = jnp.bfloat16
far_below = -1e30


def split_two(a):
    high = a.astype(bf16)
    return high, (a - high.astype(f32)).astype(bf16)


def mm(a, b):
    return lax.dot_general(a, b, (((1,), (0,)), ((), ())), preferred_element_type=f32)


def mm_nt(a, b):
    return lax.dot_general(a, b, (((1,), (1,)), ((), ())), preferred_element_type=f32)


def wide(a, b):
    n = b.shape[1]
    ah, al = split_two(a)
    bh, bl = split_two(b)
    row = jnp.concatenate([bh, bl], axis=1)
    out = mm(jnp.concatenate([ah, al], axis=1), jnp.concatenate([row, row], axis=0))
    return out[:, :n] + out[:, n:]


def wide_nt(a, b):
    n = b.shape[0]
    ah, al = split_two(a)
    bh, bl = split_two(b)
    col = jnp.concatenate([bh, bl], axis=0)
    out = mm_nt(jnp.concatenate([ah, al], axis=1), jnp.concatenate([col, col], axis=1))
    return out[:, :n] + out[:, n:]


def half_wide(a, b_half):
    ah, al = split_two(a)
    return mm(jnp.concatenate([ah, al], axis=1), jnp.concatenate([b_half, b_half], axis=0))


def local_head(q_all, k_all, v_all, d_all, logit_row, frame):
    rows, width = q_all.shape
    count = rows // frame
    scale = width ** (-0.5)
    row_at = lax.broadcasted_iota(jnp.int32, (frame, frame), 0)
    col_at = lax.broadcasted_iota(jnp.int32, (frame, frame), 1)
    diagonal = row_at == col_at
    below = row_at > col_at
    eye = jnp.where(diagonal, 1.0, 0.0).astype(f32)

    def to_row(col):
        return jnp.sum(jnp.where(diagonal, col, 0.0), axis=0, keepdims=True)

    def to_col(row):
        return jnp.sum(jnp.where(diagonal, row, 0.0), axis=1, keepdims=True)

    rate_row = 2.0 / (1.0 + jnp.exp(-logit_row))
    q, k, v, d, strict, inverse, left, right = [], [], [], [], [], [], [], []
    for f in range(count):
        at = slice(f * frame, (f + 1) * frame)
        qf, kf, vf, df = [x[at].astype(bf16) for x in (q_all, k_all, v_all, d_all)]
        d32 = d_all[at]
        s = lax.rsqrt(jnp.sum(d32 * d32, axis=1, keepdims=True) + 1e-06)
        s_row = to_row(s)
        rate = rate_row[:, at]
        gram = mm_nt(df, df)
        near = jnp.where(below, gram * (to_col(rate) * s) * s_row, 0.0)
        q.append(qf), k.append(kf), v.append(vf), d.append(df)
        strict.append(near), left.append(s), right.append(rate * s_row)
        inverse.append(eye - jnp.where((row_at // 2) == (col_at // 2), near, 0.0))
    size = 2
    while size < frame:
        corner = ((row_at // (2 * size)) == (col_at // (2 * size))) & (
            (row_at // size) != (col_at // size)
        )
        step = [wide(jnp.where(corner, strict[f], 0.0), inverse[f]) for f in range(count)]
        inverse = [inverse[f] - wide(inverse[f], step[f]) for f in range(count)]
        size *= 2
    inner, query, keys, maps = [], [], [], []
    for f in range(count):
        y = inverse[f] * left[f] * right[f]
        query_dots = jnp.where(row_at >= col_at, mm_nt(q[f], d[f]), 0.0)
        key_dots = jnp.where(row_at < col_at, mm_nt(k[f], d[f]), 0.0)
        query_mix = wide(query_dots, y)
        key_mix = wide_nt(key_dots, y)
        scores = mm_nt(q[f], k[f]) - wide_nt(query_mix, key_dots)
        inner.append(jnp.where(row_at >= col_at, scores * scale, far_below))
        query.append(q[f].astype(f32) - half_wide(query_mix, d[f]))
        keys.append(k[f].astype(f32) - half_wide(key_mix, d[f]))
        pushed = half_wide(y, d[f])
        ph, plow = split_two(pushed)
        both = mm(d[f].T, jnp.concatenate([ph, plow], axis=1))
        maps.append(eye - (both[:, :width] + both[:, width:]))
    half = [x.astype(bf16) for x in keys]
    maxima, totals, sums, block_query, block_keys = [], [], [], [], []
    for f in range(count):
        current = query[f]
        parts = [inner[f]]
        vals = [v[f]]
        for g in range(f - 1, -1, -1):
            parts.append(mm_nt(current.astype(bf16), half[g]) * scale)
            vals.append(v[g])
            current = wide(current, maps[g])
        block_query.append(current)
        top = parts[0]
        for p in parts[1:]:
            top = jnp.maximum(top, p)
        top = jnp.max(top, axis=1, keepdims=True)
        total = 0.0
        weighted = 0.0
        for p, vv in zip(parts, vals):
            w = jnp.exp(p - top)
            total = total + jnp.sum(w, axis=1, keepdims=True)
            weighted = weighted + mm(w.astype(bf16), vv)
        maxima.append(top), totals.append(total), sums.append(weighted)
    product = maps[0]
    for f in range(1, count):
        product = wide(maps[f], product)
    for g in range(count):
        moved = keys[g]
        for f in range(g + 1, count):
            moved = wide_nt(moved, maps[f])
        block_keys.append(moved)
    cat = lambda xs: jnp.concatenate(xs, axis=0)
    return (
        cat(maxima), cat(totals), cat(sums), cat(block_query), cat(block_keys).astype(bf16), product
    )


def local_kernel(groups, frame, x_ref, logit_ref, m_ref, l_ref, a_ref, q_ref, k_ref, map_ref):
    rows = [
        jnp.concatenate([x_ref[s, 0, kind].astype(f32) for s in range(groups)], axis=0)
        for kind in range(4)
    ]
    out = local_head(*rows, logit_ref[0].astype(f32), frame)
    for ref, value in zip((m_ref, l_ref, a_ref, q_ref, k_ref, map_ref), out):
        ref[0] = value


def far_kernel(groups, m_ref, l_ref, a_ref, q_ref, k_ref, v_ref, map_ref, o_ref):
    own = lax.axis_index("ctx")
    scale = q_ref.shape[-1] ** (-0.5)

    def step(i, state):
        top, total, acc, current = state
        at = own - 1 - i
        s = mm_nt(current.astype(bf16), k_ref[at, 0]) * scale
        new = jnp.maximum(top, jnp.max(s, axis=1, keepdims=True))
        factor = jnp.exp(top - new)
        w = jnp.exp(s - new)
        total = total * factor + jnp.sum(w, axis=1, keepdims=True)
        acc = acc * factor + mm(w.astype(bf16), v_ref[at, 0])
        return new, total, acc, wide(current, map_ref[at, 0])

    _, total, acc, _ = lax.fori_loop(0, own, step, (m_ref[0], l_ref[0], a_ref[0], q_ref[0]))
    out = acc / total
    n = out.shape[0] // groups
    for s in range(groups):
        o_ref[s, 0] = out[s * n : (s + 1) * n].astype(bf16)


def shards(queries, key_vectors, values, directions, beta_logit):
    groups = lax.axis_size("head")
    sections = lax.axis_size("ctx")
    local_rows, head_total, width = queries.shape
    heads = head_total // groups
    rows = local_rows * groups
    frame = 2 * SUB

    def outgoing(x):
        return x.reshape(local_rows, groups, heads, width).transpose(1, 2, 0, 3)

    stacked = jnp.stack([outgoing(x) for x in (queries, key_vectors, values, directions)], axis=2)
    arrived = lax.all_to_all(stacked, "head", 0, 0, tiled=True)
    logit = beta_logit.reshape(local_rows, groups, heads).transpose(1, 2, 0)
    logit = lax.all_to_all(logit, "head", 0, 0, tiled=True)
    logit = logit.transpose(1, 0, 2).reshape(heads, 1, rows)
    value_rows = arrived[:, :, 2].transpose(1, 0, 2, 3).reshape(heads, rows, width)
    all_values = lax.all_gather(value_rows, "ctx")

    per_head = lambda *s: pl.BlockSpec((1,) + s, lambda h: (h,) + (0,) * len(s))
    shape = lambda *s: jax.ShapeDtypeStruct((heads,) + s, f32)
    state = pl.pallas_call(
        functools.partial(local_kernel, groups, frame),
        grid=(heads,),
        in_specs=[
            pl.BlockSpec((groups, 1, 4, local_rows, width), lambda h: (0, h, 0, 0, 0)),
            per_head(1, rows),
        ],
        out_specs=[
            per_head(rows, 1), per_head(rows, 1), per_head(rows, width),
            per_head(rows, width), per_head(rows, width), per_head(width, width),
        ],
        out_shape=[
            shape(rows, 1), shape(rows, 1), shape(rows, width), shape(rows, width),
            jax.ShapeDtypeStruct((heads, rows, width), bf16), shape(width, width),
        ],
        name="local_block",
    )(arrived, logit)
    top, total, acc, query, keys, block_map = state
    all_keys = lax.all_gather(keys, "ctx")
    all_maps = lax.all_gather(block_map, "ctx")
    every = lambda *s: pl.BlockSpec((sections, 1) + s, lambda h: (0, h) + (0,) * len(s))
    out = pl.pallas_call(
        functools.partial(far_kernel, groups),
        grid=(heads,),
        in_specs=[
            per_head(rows, 1), per_head(rows, 1), per_head(rows, width), per_head(rows, width),
            every(rows, width), every(rows, width), every(width, width),
        ],
        out_specs=pl.BlockSpec((groups, 1, local_rows, width), lambda h: (0, h, 0, 0)),
        out_shape=jax.ShapeDtypeStruct((groups, heads, local_rows, width), bf16),
        name="far_blocks",
    )(top, total, acc, query, all_keys, all_values, all_maps)
    back = lax.all_to_all(out, "head", 0, 0, tiled=True)
    return back.transpose(2, 0, 1, 3).reshape(local_rows, head_total, width)


def solution(mesh):
    rows = P(("ctx", "head"), None, None)
    in_specs = (rows, rows, rows, rows, P(("ctx", "head"), None))
    return jax.shard_map(shards, mesh=mesh, in_specs=in_specs, out_specs=rows, check_vma=False)
```

```python
import functools

import jax
import jax.numpy as jnp
from jax import lax
from jax.experimental import pallas as pl
from jax.experimental.pallas import tpu as pltpu
from jax.sharding import PartitionSpec as P

SUB = 64
f32 = jnp.float32
bf16 = jnp.bfloat16
far_below = -1e30


def split_two(a):
    high = a.astype(bf16)
    return high, (a - high.astype(f32)).astype(bf16)


def mm(a, b):
    return lax.dot_general(a, b, (((1,), (0,)), ((), ())), preferred_element_type=f32)


def mm_nt(a, b):
    return lax.dot_general(a, b, (((1,), (1,)), ((), ())), preferred_element_type=f32)


def wide(a, b):
    n = b.shape[1]
    ah, al = split_two(a)
    bh, bl = split_two(b)
    row = jnp.concatenate([bh, bl], axis=1)
    out = mm(jnp.concatenate([ah, al], axis=1), jnp.concatenate([row, row], axis=0))
    return out[:, :n] + out[:, n:]


def wide_nt(a, b):
    n = b.shape[0]
    ah, al = split_two(a)
    bh, bl = split_two(b)
    col = jnp.concatenate([bh, bl], axis=0)
    out = mm_nt(jnp.concatenate([ah, al], axis=1), jnp.concatenate([col, col], axis=1))
    return out[:, :n] + out[:, n:]


def half_wide(a, b_half):
    ah, al = split_two(a)
    return mm(jnp.concatenate([ah, al], axis=1), jnp.concatenate([b_half, b_half], axis=0))


def local_head(q_all, k_all, v_all, d_all, logit_row, frame):
    rows, width = q_all.shape
    count = rows // frame
    scale = width ** (-0.5)
    row_at = lax.broadcasted_iota(jnp.int32, (frame, frame), 0)
    col_at = lax.broadcasted_iota(jnp.int32, (frame, frame), 1)
    diagonal = row_at == col_at
    below = row_at > col_at
    eye = jnp.where(diagonal, 1.0, 0.0).astype(f32)

    def to_row(col):
        return jnp.sum(jnp.where(diagonal, col, 0.0), axis=0, keepdims=True)

    def to_col(row):
        return jnp.sum(jnp.where(diagonal, row, 0.0), axis=1, keepdims=True)

    rate_row = 2.0 / (1.0 + jnp.exp(-logit_row))
    q, k, v, d, strict, inverse, left, right = [], [], [], [], [], [], [], []
    for f in range(count):
        at = slice(f * frame, (f + 1) * frame)
        qf, kf, vf, df = [x[at].astype(bf16) for x in (q_all, k_all, v_all, d_all)]
        d32 = d_all[at]
        s = lax.rsqrt(jnp.sum(d32 * d32, axis=1, keepdims=True) + 1e-06)
        s_row = to_row(s)
        rate = rate_row[:, at]
        gram = mm_nt(df, df)
        near = jnp.where(below, gram * (to_col(rate) * s) * s_row, 0.0)
        q.append(qf), k.append(kf), v.append(vf), d.append(df)
        strict.append(near), left.append(s), right.append(rate * s_row)
        inverse.append(eye - jnp.where((row_at // 2) == (col_at // 2), near, 0.0))
    size = 2
    while size < frame:
        corner = ((row_at // (2 * size)) == (col_at // (2 * size))) & (
            (row_at // size) != (col_at // size)
        )
        step = [wide(jnp.where(corner, strict[f], 0.0), inverse[f]) for f in range(count)]
        inverse = [inverse[f] - wide(inverse[f], step[f]) for f in range(count)]
        size *= 2
    inner, query, keys, maps = [], [], [], []
    for f in range(count):
        y = inverse[f] * left[f] * right[f]
        query_dots = jnp.where(row_at >= col_at, mm_nt(q[f], d[f]), 0.0)
        key_dots = jnp.where(row_at < col_at, mm_nt(k[f], d[f]), 0.0)
        query_mix = wide(query_dots, y)
        key_mix = wide_nt(key_dots, y)
        scores = mm_nt(q[f], k[f]) - wide_nt(query_mix, key_dots)
        inner.append(jnp.where(row_at >= col_at, scores * scale, far_below))
        query.append(q[f].astype(f32) - half_wide(query_mix, d[f]))
        keys.append(k[f].astype(f32) - half_wide(key_mix, d[f]))
        pushed = half_wide(y, d[f])
        ph, plow = split_two(pushed)
        both = mm(d[f].T, jnp.concatenate([ph, plow], axis=1))
        maps.append(eye - (both[:, :width] + both[:, width:]))
    half = [x.astype(bf16) for x in keys]
    maxima, totals, sums, block_query, block_keys = [], [], [], [], []
    for f in range(count):
        current = query[f]
        parts = [inner[f]]
        vals = [v[f]]
        for g in range(f - 1, -1, -1):
            parts.append(mm_nt(current.astype(bf16), half[g]) * scale)
            vals.append(v[g])
            current = wide(current, maps[g])
        block_query.append(current)
        top = parts[0]
        for p in parts[1:]:
            top = jnp.maximum(top, p)
        top = jnp.max(top, axis=1, keepdims=True)
        total = 0.0
        weighted = 0.0
        for p, vv in zip(parts, vals):
            w = jnp.exp(p - top)
            total = total + jnp.sum(w, axis=1, keepdims=True)
            weighted = weighted + mm(w.astype(bf16), vv)
        maxima.append(top), totals.append(total), sums.append(weighted)
    product = maps[0]
    for f in range(1, count):
        product = wide(maps[f], product)
    for g in range(count):
        moved = keys[g]
        for f in range(g + 1, count):
            moved = wide_nt(moved, maps[f])
        block_keys.append(moved)
    cat = lambda xs: jnp.concatenate(xs, axis=0)
    return (
        cat(maxima), cat(totals), cat(sums), cat(block_query), cat(block_keys), product
    )


KEYS, VALUES, MAPS = 0, 1, 2
MESH = pl.DeviceIdType.MESH


def block_kernel(
    groups, levels, frame, x_ref, v_ref, logit_ref, o_ref,
    kv_buf, map_buf, key_self, key_wide, query, acc, top, total, own_map, side_map,
    send_on, send_side, arrive, pair_send, pair_arrive,
):
    heads, rows, width = v_ref.shape
    part = map_buf.shape[2]
    scale = width ** (-0.5)
    own = lax.axis_index("ctx")
    level = own // 2
    core = own % 2
    onward, back, side = own + 2, own - 2, own + 1 - 2 * core
    has_next = level < levels - 1
    has_map = has_next & (level >= 1)
    barrier = pltpu.get_barrier_semaphore()

    def greet(at):
        pl.semaphore_signal(barrier, inc=1, device_id={"ctx": at}, device_id_type=MESH)

    greet(side)

    @pl.when(has_next)
    def _():
        greet(onward)

    @pl.when(level >= 1)
    def _():
        greet(back)

    pl.semaphore_wait(barrier, 1 + has_next.astype(jnp.int32) + (level >= 1).astype(jnp.int32))

    def slot(at, column, kind):
        return map_buf.at[at, column] if kind == MAPS else kv_buf.at[at, column, kind]

    def copy(source, at, kind, target, send):
        return pltpu.make_async_remote_copy(
            src_ref=source,
            dst_ref=slot(at, core, kind),
            send_sem=send.at[at, kind],
            recv_sem=arrive.at[at, core, kind],
            device_id={"ctx": target},
            device_id_type=MESH,
        )

    def send_next(source, at, kind):
        copy(source, at, kind, onward, send_on).start()

    def await_slot(at, column, kind):
        pltpu.make_async_remote_copy(
            src_ref=slot(at, column, kind),
            dst_ref=slot(at, column, kind),
            send_sem=send_side.at[at, kind],
            recv_sem=arrive.at[at, column, kind],
            device_id={"ctx": side},
            device_id_type=MESH,
        ).wait_recv()

    def relay(at, kind):
        await_slot(at, core, kind)

        @pl.when(has_next)
        def _():
            send_next(slot(at, core, kind), at, kind)

        copy(slot(at, core, kind), at, kind, side, send_side).start()

    @pl.when(has_next)
    def _():
        send_next(v_ref, level, VALUES)

    @pl.when(core == 0)
    def _():
        copy(v_ref, level, VALUES, side, send_side).start()

    def local(h, carry):
        pieces = [
            jnp.concatenate([x_ref[s, h, kind].astype(f32) for s in range(groups)], axis=0)
            for kind in range(4)
        ]
        m, l, a, q, k, moved = local_head(*pieces, logit_ref[h].astype(f32), frame)
        top[h] = m
        total[h] = l
        acc[h] = a
        query[h] = q
        key_wide[h] = k
        key_self[h] = k.astype(bf16)
        own_map[h] = moved
        return carry

    lax.fori_loop(0, heads // 2, local, 0)

    @pl.when(level >= 1)
    def _():
        relay(level - 1, VALUES)

    lax.fori_loop(heads // 2, heads, local, 0)

    swap = pltpu.make_async_remote_copy(
        src_ref=own_map,
        dst_ref=side_map,
        send_sem=pair_send,
        recv_sem=pair_arrive,
        device_id={"ctx": side},
        device_id_type=MESH,
    )
    swap.start()

    @pl.when((core == 1) & has_next)
    def _():
        send_next(key_self, level, KEYS)

    @pl.when(core == 0)
    def _():
        copy(key_self, level, KEYS, side, send_side).start()

    @pl.when(level >= 2)
    def _():
        relay(level - 2, VALUES)

    swap.wait_recv()

    @pl.when((core == 0) & has_next)
    def _():
        def rebase(h, carry):
            kv_buf[level, 0, KEYS, h] = wide_nt(key_wide[h], side_map[h]).astype(bf16)
            return carry

        lax.fori_loop(0, heads, rebase, 0)
        send_next(slot(level, 0, KEYS), level, KEYS)

    @pl.when(has_map & (core == 0))
    def _():
        for i in range(part):
            map_buf[level, 0, i] = wide(side_map[i], own_map[i])

    @pl.when(has_map & (core == 1))
    def _():
        for i in range(part):
            map_buf[level, 1, i] = wide(own_map[part + i], side_map[part + i])

    @pl.when(has_map)
    def _():
        send_next(slot(level, core, MAPS), level, MAPS)

    def absorb(h, pieces):
        current = query[h].astype(bf16)
        scores = [mm_nt(current, kv_buf[at, c, KEYS, h]) * scale for at, c in pieces]
        new = top[h]
        for s in scores:
            new = jnp.maximum(new, jnp.max(s, axis=1, keepdims=True))
        factor = jnp.exp(top[h] - new)
        amount = total[h] * factor
        weighted = acc[h] * factor
        for s, (at, c) in zip(scores, pieces):
            w = jnp.exp(s - new)
            amount = amount + jnp.sum(w, axis=1, keepdims=True)
            weighted = weighted + mm(w.astype(bf16), kv_buf[at, c, VALUES, h])
        top[h] = new
        total[h] = amount
        acc[h] = weighted

    @pl.when(core == 1)
    def _():
        await_slot(level, 0, VALUES)
        await_slot(level, 0, KEYS)

        def near(h, carry):
            absorb(h, [(level, 0)])
            query[h] = wide(query[h], side_map[h])
            return carry

        lax.fori_loop(0, heads, near, 0)

    def far(i, carry):
        at = level - 1 - i

        @pl.when(i >= 2)
        def _():
            relay(at, VALUES)

        relay(at, KEYS)

        @pl.when(at >= 1)
        def _():
            relay(at, MAPS)

        await_slot(at, 1 - core, VALUES)
        await_slot(at, 1 - core, KEYS)

        def one(h, inner):
            absorb(h, [(at, 1), (at, 0)])
            return inner

        lax.fori_loop(0, heads, one, 0)

        @pl.when(at >= 1)
        def _():
            await_slot(at, 1 - core, MAPS)

            def move(h, inner):
                query[h] = wide(query[h], map_buf[at, h // part, h % part])
                return inner

            lax.fori_loop(0, heads, move, 0)

        return carry

    lax.fori_loop(0, level, far, 0)

    def finish(h, carry):
        out = acc[h] / total[h]
        n = rows // groups
        for s in range(groups):
            o_ref[s, h] = out[s * n : (s + 1) * n].astype(bf16)
        return carry

    lax.fori_loop(0, heads, finish, 0)

    def settle(at, kind, target, send):
        copy(slot(at, core, kind), at, kind, target, send).wait_send()

    def settle_side(at, carry):
        settle(at, KEYS, side, send_side)
        settle(at, VALUES, side, send_side)

        @pl.when(at >= 1)
        def _():
            settle(at, MAPS, side, send_side)

        return carry

    def settle_next(at, carry):
        settle(at, KEYS, onward, send_on)
        settle(at, VALUES, onward, send_on)

        @pl.when(at >= 1)
        def _():
            settle(at, MAPS, onward, send_on)

        return carry

    lax.fori_loop(0, level, settle_side, 0)

    @pl.when(core == 0)
    def _():
        settle(level, KEYS, side, send_side)
        settle(level, VALUES, side, send_side)

    @pl.when(has_next)
    def _():
        lax.fori_loop(0, level + 1, settle_next, 0)

    swap.wait_send()


def shards(queries, key_vectors, values, directions, beta_logit):
    groups = lax.axis_size("head")
    levels = lax.axis_size("ctx") // 2
    local_rows, head_total, width = queries.shape
    heads = head_total // groups
    rows = local_rows * groups

    def outgoing(x):
        return x.reshape(local_rows, groups, heads, width).transpose(1, 2, 0, 3)

    stacked = jnp.stack([outgoing(x) for x in (queries, key_vectors, values, directions)], axis=2)
    arrived = lax.all_to_all(stacked, "head", 0, 0, tiled=True)
    logit = beta_logit.reshape(local_rows, groups, heads).transpose(1, 2, 0)
    logit = lax.all_to_all(logit, "head", 0, 0, tiled=True)
    logit = logit.transpose(1, 0, 2).reshape(heads, 1, rows)
    value_rows = arrived[:, :, 2].transpose(1, 0, 2, 3).reshape(heads, rows, width)
    part = heads // 2
    vmem = pl.BlockSpec(memory_space=pltpu.VMEM)
    out = pl.pallas_call(
        functools.partial(block_kernel, groups, levels, 2 * SUB),
        in_specs=[vmem] * 3,
        out_specs=vmem,
        out_shape=jax.ShapeDtypeStruct((groups, heads, local_rows, width), bf16),
        scratch_shapes=[
            pltpu.VMEM((levels, 2, 2, heads, rows, width), bf16),
            pltpu.VMEM((levels, 2, part, width, width), f32),
            pltpu.VMEM((heads, rows, width), bf16),
            pltpu.VMEM((heads, rows, width), f32),
            pltpu.VMEM((heads, rows, width), f32),
            pltpu.VMEM((heads, rows, width), f32),
            pltpu.VMEM((heads, rows, 1), f32),
            pltpu.VMEM((heads, rows, 1), f32),
            pltpu.VMEM((heads, width, width), f32),
            pltpu.VMEM((heads, width, width), f32),
            pltpu.SemaphoreType.DMA((levels, 3)),
            pltpu.SemaphoreType.DMA((levels, 3)),
            pltpu.SemaphoreType.DMA((levels, 2, 3)),
            pltpu.SemaphoreType.DMA,
            pltpu.SemaphoreType.DMA,
        ],
        compiler_params=pltpu.CompilerParams(collective_id=0, has_side_effects=True),
        name="block_chain",
    )(arrived, value_rows, logit)
    back = lax.all_to_all(out, "head", 0, 0, tiled=True)
    return back.transpose(2, 0, 1, 3).reshape(local_rows, head_total, width)


def solution(mesh):
    rows = P(("ctx", "head"), None, None)
    in_specs = (rows, rows, rows, rows, P(("ctx", "head"), None))
    return jax.shard_map(shards, mesh=mesh, in_specs=in_specs, out_specs=rows, check_vma=False)
```

```python
import functools

import jax
import jax.numpy as jnp
from jax import lax
from jax.experimental import pallas as pl
from jax.experimental.pallas import tpu as pltpu
from jax.sharding import PartitionSpec as P

SUB = 64
f32 = jnp.float32
bf16 = jnp.bfloat16
far_below = -1e30


def split_two(a):
    high = a.astype(bf16)
    return high, (a - high.astype(f32)).astype(bf16)


def mm(a, b):
    return lax.dot_general(a, b, (((1,), (0,)), ((), ())), preferred_element_type=f32)


def mm_nt(a, b):
    return lax.dot_general(a, b, (((1,), (1,)), ((), ())), preferred_element_type=f32)


def wide(a, b):
    n = b.shape[1]
    ah, al = split_two(a)
    bh, bl = split_two(b)
    row = jnp.concatenate([bh, bl], axis=1)
    out = mm(jnp.concatenate([ah, al], axis=1), jnp.concatenate([row, row], axis=0))
    return out[:, :n] + out[:, n:]


def wide_nt(a, b):
    n = b.shape[0]
    ah, al = split_two(a)
    bh, bl = split_two(b)
    col = jnp.concatenate([bh, bl], axis=0)
    out = mm_nt(jnp.concatenate([ah, al], axis=1), jnp.concatenate([col, col], axis=1))
    return out[:, :n] + out[:, n:]


def half_wide(a, b_half):
    ah, al = split_two(a)
    return mm(jnp.concatenate([ah, al], axis=1), jnp.concatenate([b_half, b_half], axis=0))


def local_head(q_all, k_all, v_all, d_all, logit_col, frame):
    rows, width = q_all.shape
    count = rows // frame
    scale = width ** (-0.5)
    row_at = lax.broadcasted_iota(jnp.int32, (frame, frame), 0)
    col_at = lax.broadcasted_iota(jnp.int32, (frame, frame), 1)
    diagonal = row_at == col_at
    below = row_at > col_at
    eye = jnp.where(diagonal, 1.0, 0.0).astype(f32)

    def to_row(col):
        return jnp.sum(jnp.where(diagonal, col, 0.0), axis=0, keepdims=True)

    rate_col = 2.0 / (1.0 + jnp.exp(-logit_col))
    q, k, v, d, strict, inverse, left, right = [], [], [], [], [], [], [], []
    for f in range(count):
        at = slice(f * frame, (f + 1) * frame)
        qf, kf, vf, df = [x[at].astype(bf16) for x in (q_all, k_all, v_all, d_all)]
        d32 = d_all[at]
        s = lax.rsqrt(jnp.sum(d32 * d32, axis=1, keepdims=True) + 1e-06)
        s_row = to_row(s)
        rate = rate_col[at]
        gram = mm_nt(df, df)
        near = jnp.where(below, gram * (rate * s) * s_row, 0.0)
        q.append(qf), k.append(kf), v.append(vf), d.append(df)
        strict.append(near), left.append(s), right.append(to_row(rate * s))
        inverse.append(eye - jnp.where((row_at // 2) == (col_at // 2), near, 0.0))
    size = 2
    while size < frame:
        corner = ((row_at // (2 * size)) == (col_at // (2 * size))) & (
            (row_at // size) != (col_at // size)
        )
        step = [wide(jnp.where(corner, strict[f], 0.0), inverse[f]) for f in range(count)]
        inverse = [inverse[f] - wide(inverse[f], step[f]) for f in range(count)]
        size *= 2
    inner, query, keys, maps = [], [], [], []
    for f in range(count):
        y = inverse[f] * left[f] * right[f]
        query_dots = jnp.where(row_at >= col_at, mm_nt(q[f], d[f]), 0.0)
        key_dots = jnp.where(row_at < col_at, mm_nt(k[f], d[f]), 0.0)
        query_mix = wide(query_dots, y)
        key_mix = wide_nt(key_dots, y)
        scores = mm_nt(q[f], k[f]) - wide_nt(query_mix, key_dots)
        inner.append(jnp.where(row_at >= col_at, scores * scale, far_below))
        query.append(q[f].astype(f32) - half_wide(query_mix, d[f]))
        keys.append(k[f].astype(f32) - half_wide(key_mix, d[f]))
        pushed = half_wide(y, d[f])
        ph, plow = split_two(pushed)
        both = mm(d[f].T, jnp.concatenate([ph, plow], axis=1))
        maps.append(eye - (both[:, :width] + both[:, width:]))
    half = [x.astype(bf16) for x in keys]
    maxima, totals, sums, block_query, block_keys = [], [], [], [], []
    for f in range(count):
        current = query[f]
        parts = [inner[f]]
        vals = [v[f]]
        for g in range(f - 1, -1, -1):
            parts.append(mm_nt(current.astype(bf16), half[g]) * scale)
            vals.append(v[g])
            current = wide(current, maps[g])
        block_query.append(current)
        top = parts[0]
        for p in parts[1:]:
            top = jnp.maximum(top, p)
        top = jnp.max(top, axis=1, keepdims=True)
        total = 0.0
        weighted = 0.0
        for p, vv in zip(parts, vals):
            w = jnp.exp(p - top)
            total = total + jnp.sum(w, axis=1, keepdims=True)
            weighted = weighted + mm(w.astype(bf16), vv)
        maxima.append(top), totals.append(total), sums.append(weighted)
    product = maps[0]
    for f in range(1, count):
        product = wide(maps[f], product)
    for g in range(count):
        moved = keys[g]
        for f in range(g + 1, count):
            moved = wide_nt(moved, maps[f])
        block_keys.append(moved)
    cat = lambda xs: jnp.concatenate(xs, axis=0)
    return (
        cat(maxima), cat(totals), cat(sums), cat(block_query), cat(block_keys), product
    )


KEYS, VALUES, MAPS = 0, 1, 2
MESH = pl.DeviceIdType.MESH


def block_kernel(
    groups, levels, frame, chunks, x_ref, v_ref, logit_ref, o_ref,
    x_in, logit_in, out_buf,
    key_buf, value_buf, map_buf, key_self, key_wide, query, acc, top, total, own_map, side_map,
    send_on, send_side, arrive, pair_send, pair_arrive,
    x_send, x_arrive, v_send, v_arrive, b_send, b_arrive, o_send, o_arrive, keep,
):
    _, heads, local_rows, width = v_ref.shape
    rows = groups * local_rows
    chunk = heads // chunks
    part = map_buf.shape[2]
    scale = width ** (-0.5)
    own = lax.axis_index("ctx")
    me = lax.axis_index("head")
    level = own // 2
    core = own % 2
    onward, back, side = own + 2, own - 2, own + 1 - 2 * core
    has_next = level < levels - 1
    has_map = has_next & (level >= 1)
    barrier = pltpu.get_barrier_semaphore()

    def greet(at):
        pl.semaphore_signal(barrier, inc=1, device_id={"ctx": at}, device_id_type=MESH)

    greet(side)

    @pl.when(has_next)
    def _():
        greet(onward)

    @pl.when(level >= 1)
    def _():
        greet(back)

    for p in range(1, groups):
        peer = (me + p) % groups
        pl.semaphore_signal(barrier, inc=1, device_id={"head": peer}, device_id_type=MESH)
    pl.semaphore_wait(
        barrier, groups + has_next.astype(jnp.int32) + (level >= 1).astype(jnp.int32)
    )

    def across(source, target, p, send, recv):
        return pltpu.make_async_remote_copy(
            src_ref=source,
            dst_ref=target,
            send_sem=send,
            recv_sem=recv,
            device_id={"head": (me + p) % groups},
            device_id_type=MESH,
        )

    def v_copy(p):
        to = value_buf.at[level, core, :, me]
        return across(v_ref.at[(me + p) % groups], to, p, v_send.at[p], v_arrive.at[p])

    def b_copy(p):
        to = logit_in.at[me]
        return across(logit_ref.at[(me + p) % groups], to, p, b_send.at[p], b_arrive.at[p])

    def x_copy(p, c):
        at = pl.ds(c * chunk, chunk)
        source = x_ref.at[(me + p) % groups, at]
        return across(source, x_in.at[me, at], p, x_send.at[p, c], x_arrive.at[p, c])

    def o_copy(p, h):
        source = out_buf.at[(me + p) % groups, h]
        return across(source, o_ref.at[me, h], p, o_send.at[p, h], o_arrive.at[p, h])

    kept = [
        pltpu.make_async_copy(v_ref.at[me], value_buf.at[level, core, :, me], keep.at[0]),
        pltpu.make_async_copy(logit_ref.at[me], logit_in.at[me], keep.at[1]),
        pltpu.make_async_copy(x_ref.at[me], x_in.at[me], keep.at[2]),
    ]
    for p in range(1, groups):
        b_copy(p).start()
        v_copy(p).start()
    for c in range(chunks):
        for p in range(1, groups):
            x_copy(p, c).start()
    for one_copy in kept:
        one_copy.start()
    for p in range(1, groups):
        b_copy(p).wait_recv()
        v_copy(p).wait_recv()
    for one_copy in kept:
        one_copy.wait()
    v_own = value_buf.at[level, core]

    def value_rows(at, c, h):
        if local_rows % 16 == 0:
            return value_buf[at, c, h].reshape(rows, width)
        pieces = [value_buf[at, c, h, s].astype(f32) for s in range(groups)]
        return jnp.concatenate(pieces, axis=0).astype(bf16)

    def slot(at, column, kind):
        return (key_buf, value_buf, map_buf)[kind].at[at, column]

    def copy(source, at, kind, target, send):
        return pltpu.make_async_remote_copy(
            src_ref=source,
            dst_ref=slot(at, core, kind),
            send_sem=send.at[at, kind],
            recv_sem=arrive.at[at, core, kind],
            device_id={"ctx": target},
            device_id_type=MESH,
        )

    def send_next(source, at, kind):
        copy(source, at, kind, onward, send_on).start()

    def await_slot(at, column, kind):
        pltpu.make_async_remote_copy(
            src_ref=slot(at, column, kind),
            dst_ref=slot(at, column, kind),
            send_sem=send_side.at[at, kind],
            recv_sem=arrive.at[at, column, kind],
            device_id={"ctx": side},
            device_id_type=MESH,
        ).wait_recv()

    def relay(at, kind):
        await_slot(at, core, kind)

        @pl.when(has_next)
        def _():
            send_next(slot(at, core, kind), at, kind)

        copy(slot(at, core, kind), at, kind, side, send_side).start()

    @pl.when(has_next)
    def _():
        send_next(v_own, level, VALUES)

    @pl.when(core == 0)
    def _():
        copy(v_own, level, VALUES, side, send_side).start()

    at_row = lax.broadcasted_iota(jnp.int32, (local_rows, local_rows), 0)
    at_col = lax.broadcasted_iota(jnp.int32, (local_rows, local_rows), 1)

    def upright(row):
        return jnp.sum(jnp.where(at_row == at_col, row, 0.0), axis=1, keepdims=True)

    def local(h, carry):
        joined = lambda xs: jnp.concatenate(xs, axis=0)
        q0, k0, d0 = [
            joined([x_in[s, h, kind].astype(f32) for s in range(groups)]) for kind in range(3)
        ]
        v0 = value_rows(level, core, h)
        logit = joined([upright(logit_in[s, pl.ds(h, 1), :]) for s in range(groups)])
        m, l, a, q, k, moved = local_head(q0, k0, v0, d0, logit, frame)
        top[h] = m
        total[h] = l
        acc[h] = a
        query[h] = q
        key_wide[h] = k
        key_self[h] = k.astype(bf16)
        own_map[h] = moved
        return carry

    for c in range(chunks):
        for p in range(1, groups):
            x_copy(p, c).wait_recv()
        lax.fori_loop(c * chunk, (c + 1) * chunk, local, 0)
        if c == (chunks - 1) // 2:

            @pl.when(level >= 1)
            def _():
                relay(level - 1, VALUES)

    swap = pltpu.make_async_remote_copy(
        src_ref=own_map,
        dst_ref=side_map,
        send_sem=pair_send,
        recv_sem=pair_arrive,
        device_id={"ctx": side},
        device_id_type=MESH,
    )
    swap.start()

    @pl.when((core == 1) & has_next)
    def _():
        send_next(key_self, level, KEYS)

    @pl.when(core == 0)
    def _():
        copy(key_self, level, KEYS, side, send_side).start()

    @pl.when(level >= 2)
    def _():
        relay(level - 2, VALUES)

    swap.wait_recv()

    @pl.when((core == 0) & has_next)
    def _():
        def rebase(h, carry):
            key_buf[level, 0, h] = wide_nt(key_wide[h], side_map[h]).astype(bf16)
            return carry

        lax.fori_loop(0, heads, rebase, 0)
        send_next(slot(level, 0, KEYS), level, KEYS)

    @pl.when(has_map & (core == 0))
    def _():
        for i in range(part):
            map_buf[level, 0, i] = wide(side_map[i], own_map[i])

    @pl.when(has_map & (core == 1))
    def _():
        for i in range(part):
            map_buf[level, 1, i] = wide(own_map[part + i], side_map[part + i])

    @pl.when(has_map)
    def _():
        send_next(slot(level, core, MAPS), level, MAPS)

    def absorb(h, pieces):
        current = query[h].astype(bf16)
        scores = [mm_nt(current, key_buf[at, c, h]) * scale for at, c in pieces]
        new = top[h]
        for s in scores:
            new = jnp.maximum(new, jnp.max(s, axis=1, keepdims=True))
        factor = jnp.exp(top[h] - new)
        amount = total[h] * factor
        weighted = acc[h] * factor
        for s, (at, c) in zip(scores, pieces):
            w = jnp.exp(s - new)
            amount = amount + jnp.sum(w, axis=1, keepdims=True)
            weighted = weighted + mm(w.astype(bf16), value_rows(at, c, h))
        top[h] = new
        total[h] = amount
        acc[h] = weighted

    def finish(h):
        out = acc[h] / total[h]
        for s in range(groups):
            piece = out[s * local_rows : (s + 1) * local_rows].astype(bf16)
            out_buf[s, h] = piece

    def hand_back(h):
        for p in range(1, groups):
            o_copy(p, h).start()

    def close(h):
        finish(h)

        @pl.when(h >= 1)
        def _():
            hand_back(h - 1)

    @pl.when(core == 1)
    def _():
        await_slot(level, 0, VALUES)
        await_slot(level, 0, KEYS)

        def near(h, carry):
            absorb(h, [(level, 0)])
            query[h] = wide(query[h], side_map[h])
            return carry

        lax.fori_loop(0, heads, near, 0)

    def far(i, carry):
        at = level - 1 - i

        @pl.when(i >= 2)
        def _():
            relay(at, VALUES)

        relay(at, KEYS)

        @pl.when(at >= 1)
        def _():
            relay(at, MAPS)

        await_slot(at, 1 - core, VALUES)
        await_slot(at, 1 - core, KEYS)

        def one(h, inner):
            absorb(h, [(at, 1), (at, 0)])

            @pl.when(at == 0)
            def _():
                close(h)

            return inner

        lax.fori_loop(0, heads, one, 0)

        @pl.when(at >= 1)
        def _():
            await_slot(at, 1 - core, MAPS)

            def move(h, inner):
                query[h] = wide(query[h], map_buf[at, h // part, h % part])
                return inner

            lax.fori_loop(0, heads, move, 0)

        return carry

    lax.fori_loop(0, level, far, 0)

    @pl.when(level == 0)
    def _():
        def last(h, carry):
            close(h)
            return carry

        lax.fori_loop(0, heads, last, 0)

    o_ref[me] = out_buf[me]
    hand_back(heads - 1)

    def settle(at, kind, target, send):
        copy(slot(at, core, kind), at, kind, target, send).wait_send()

    def settle_side(at, carry):
        settle(at, KEYS, side, send_side)
        settle(at, VALUES, side, send_side)

        @pl.when(at >= 1)
        def _():
            settle(at, MAPS, side, send_side)

        return carry

    def settle_next(at, carry):
        settle(at, KEYS, onward, send_on)
        settle(at, VALUES, onward, send_on)

        @pl.when(at >= 1)
        def _():
            settle(at, MAPS, onward, send_on)

        return carry

    lax.fori_loop(0, level, settle_side, 0)

    @pl.when(core == 0)
    def _():
        settle(level, KEYS, side, send_side)
        settle(level, VALUES, side, send_side)

    @pl.when(has_next)
    def _():
        lax.fori_loop(0, level + 1, settle_next, 0)

    swap.wait_send()
    for p in range(1, groups):
        b_copy(p).wait_send()
        v_copy(p).wait_send()
        for c in range(chunks):
            x_copy(p, c).wait_send()

        def handed(h, carry):
            o_copy(p, h).wait()
            return carry

        lax.fori_loop(0, heads, handed, 0)


def shards(queries, key_vectors, values, directions, beta_logit):
    groups = lax.axis_size("head")
    levels = lax.axis_size("ctx") // 2
    local_rows, head_total, width = queries.shape
    heads = head_total // groups
    rows = local_rows * groups

    def outgoing(x):
        return x.reshape(local_rows, groups, heads, width).transpose(1, 2, 0, 3)

    stacked = jnp.stack([outgoing(x) for x in (queries, key_vectors, directions)], axis=2)
    value_rows = outgoing(values)
    logit = beta_logit.reshape(local_rows, groups, heads).transpose(1, 2, 0).astype(f32)
    chunks = 4 if heads % 4 == 0 else heads
    part = heads // 2
    vmem = pl.BlockSpec(memory_space=pltpu.VMEM)
    out = pl.pallas_call(
        functools.partial(block_kernel, groups, levels, 2 * SUB, chunks),
        in_specs=[vmem] * 3,
        out_specs=vmem,
        out_shape=jax.ShapeDtypeStruct((groups, heads, local_rows, width), bf16),
        scratch_shapes=[
            pltpu.VMEM(stacked.shape, bf16),
            pltpu.VMEM(logit.shape, f32),
            pltpu.VMEM((groups, heads, local_rows, width), bf16),
            pltpu.VMEM((levels, 2, heads, rows, width), bf16),
            pltpu.VMEM((levels, 2, heads, groups, local_rows, width), bf16),
            pltpu.VMEM((levels, 2, part, width, width), f32),
            pltpu.VMEM((heads, rows, width), bf16),
            pltpu.VMEM((heads, rows, width), f32),
            pltpu.VMEM((heads, rows, width), f32),
            pltpu.VMEM((heads, rows, width), f32),
            pltpu.VMEM((heads, rows, 1), f32),
            pltpu.VMEM((heads, rows, 1), f32),
            pltpu.VMEM((heads, width, width), f32),
            pltpu.VMEM((heads, width, width), f32),
            pltpu.SemaphoreType.DMA((levels, 3)),
            pltpu.SemaphoreType.DMA((levels, 3)),
            pltpu.SemaphoreType.DMA((levels, 2, 3)),
            pltpu.SemaphoreType.DMA,
            pltpu.SemaphoreType.DMA,
            pltpu.SemaphoreType.DMA((groups, chunks)),
            pltpu.SemaphoreType.DMA((groups, chunks)),
            pltpu.SemaphoreType.DMA((groups,)),
            pltpu.SemaphoreType.DMA((groups,)),
            pltpu.SemaphoreType.DMA((groups,)),
            pltpu.SemaphoreType.DMA((groups,)),
            pltpu.SemaphoreType.DMA((groups, heads)),
            pltpu.SemaphoreType.DMA((groups, heads)),
            pltpu.SemaphoreType.DMA((3,)),
        ],
        compiler_params=pltpu.CompilerParams(collective_id=0, has_side_effects=True),
        name="block_chain",
    )(stacked, value_rows, logit)
    return out.transpose(2, 0, 1, 3).reshape(local_rows, head_total, width)


def solution(mesh):
    rows = P(("ctx", "head"), None, None)
    in_specs = (rows, rows, rows, rows, P(("ctx", "head"), None))
    return jax.shard_map(shards, mesh=mesh, in_specs=in_specs, out_specs=rows, check_vma=False)
```

```python
import functools

import jax
import jax.numpy as jnp
from jax import lax
from jax.experimental import pallas as pl
from jax.experimental.pallas import tpu as pltpu
from jax.sharding import PartitionSpec as P

SUB = 64
f32 = jnp.float32
bf16 = jnp.bfloat16
far_below = -1e30


def split_two(a):
    high = a.astype(bf16)
    return high, (a - high.astype(f32)).astype(bf16)


def mm(a, b):
    return lax.dot_general(a, b, (((1,), (0,)), ((), ())), preferred_element_type=f32)


def mm_nt(a, b):
    return lax.dot_general(a, b, (((1,), (1,)), ((), ())), preferred_element_type=f32)


def wide(a, b):
    n = b.shape[1]
    ah, al = split_two(a)
    bh, bl = split_two(b)
    row = jnp.concatenate([bh, bl], axis=1)
    out = mm(jnp.concatenate([ah, al], axis=1), jnp.concatenate([row, row], axis=0))
    return out[:, :n] + out[:, n:]


def wide_nt(a, b):
    n = b.shape[0]
    ah, al = split_two(a)
    bh, bl = split_two(b)
    col = jnp.concatenate([bh, bl], axis=0)
    out = mm_nt(jnp.concatenate([ah, al], axis=1), jnp.concatenate([col, col], axis=1))
    return out[:, :n] + out[:, n:]


def half_wide(a, b_half):
    ah, al = split_two(a)
    return mm(jnp.concatenate([ah, al], axis=1), jnp.concatenate([b_half, b_half], axis=0))


def local_head(q_all, k_all, v_all, d_all, logit_col, frame):
    rows, width = q_all.shape
    count = rows // frame
    scale = width ** (-0.5)
    row_at = lax.broadcasted_iota(jnp.int32, (frame, frame), 0)
    col_at = lax.broadcasted_iota(jnp.int32, (frame, frame), 1)
    diagonal = row_at == col_at
    below = row_at > col_at
    eye = jnp.where(diagonal, 1.0, 0.0).astype(f32)

    def to_row(col):
        return jnp.sum(jnp.where(diagonal, col, 0.0), axis=0, keepdims=True)

    rate_col = 2.0 / (1.0 + jnp.exp(-logit_col))
    q, k, v, d, strict, inverse, left, right = [], [], [], [], [], [], [], []
    for f in range(count):
        at = slice(f * frame, (f + 1) * frame)
        qf, kf, vf, df = [x[at].astype(bf16) for x in (q_all, k_all, v_all, d_all)]
        d32 = d_all[at]
        s = lax.rsqrt(jnp.sum(d32 * d32, axis=1, keepdims=True) + 1e-06)
        s_row = to_row(s)
        rate = rate_col[at]
        gram = mm_nt(df, df)
        near = jnp.where(below, gram * (rate * s) * s_row, 0.0)
        q.append(qf), k.append(kf), v.append(vf), d.append(df)
        strict.append(near), left.append(s), right.append(to_row(rate * s))
        inverse.append(eye - jnp.where((row_at // 2) == (col_at // 2), near, 0.0))
    size = 2
    while size < frame:
        corner = ((row_at // (2 * size)) == (col_at // (2 * size))) & (
            (row_at // size) != (col_at // size)
        )
        step = [wide(jnp.where(corner, strict[f], 0.0), inverse[f]) for f in range(count)]
        inverse = [inverse[f] - wide(inverse[f], step[f]) for f in range(count)]
        size *= 2
    inner, query, keys, maps = [], [], [], []
    for f in range(count):
        y = inverse[f] * left[f] * right[f]
        query_dots = jnp.where(row_at >= col_at, mm_nt(q[f], d[f]), 0.0)
        key_dots = jnp.where(row_at < col_at, mm_nt(k[f], d[f]), 0.0)
        query_mix = wide(query_dots, y)
        key_mix = wide_nt(key_dots, y)
        scores = mm_nt(q[f], k[f]) - wide_nt(query_mix, key_dots)
        inner.append(jnp.where(row_at >= col_at, scores * scale, far_below))
        query.append(q[f].astype(f32) - half_wide(query_mix, d[f]))
        keys.append(k[f].astype(f32) - half_wide(key_mix, d[f]))
        pushed = half_wide(y, d[f])
        ph, plow = split_two(pushed)
        both = mm(d[f].T, jnp.concatenate([ph, plow], axis=1))
        maps.append(eye - (both[:, :width] + both[:, width:]))
    half = [x.astype(bf16) for x in keys]
    maxima, totals, sums, block_query, block_keys = [], [], [], [], []
    for f in range(count):
        current = query[f]
        parts = [inner[f]]
        vals = [v[f]]
        for g in range(f - 1, -1, -1):
            parts.append(mm_nt(current.astype(bf16), half[g]) * scale)
            vals.append(v[g])
            current = wide(current, maps[g])
        block_query.append(current)
        top = parts[0]
        for p in parts[1:]:
            top = jnp.maximum(top, p)
        top = jnp.max(top, axis=1, keepdims=True)
        total = 0.0
        weighted = 0.0
        for p, vv in zip(parts, vals):
            w = jnp.exp(p - top)
            total = total + jnp.sum(w, axis=1, keepdims=True)
            weighted = weighted + mm(w.astype(bf16), vv)
        maxima.append(top), totals.append(total), sums.append(weighted)
    product = maps[0]
    for f in range(1, count):
        product = wide(maps[f], product)
    for g in range(count):
        moved = keys[g]
        for f in range(g + 1, count):
            moved = wide_nt(moved, maps[f])
        block_keys.append(moved)
    cat = lambda xs: jnp.concatenate(xs, axis=0)
    return (
        cat(maxima), cat(totals), cat(sums), cat(block_query), cat(block_keys), product
    )


VALUES, MAPS, KEYS = 0, 1, 2
MESH = pl.DeviceIdType.MESH


def block_kernel(
    groups, levels, frame, chunks, x_ref, v_ref, logit_ref, o_ref,
    x_in, logit_in, out_buf,
    key_buf, value_buf, map_buf, key_self, key_wide, query, acc, top, total, own_map, side_map,
    send_on, send_side, arrive, pair_send, pair_arrive,
    x_send, x_arrive, v_send, v_arrive, b_send, b_arrive, o_send, o_arrive, keep,
):
    _, heads, local_rows, width = v_ref.shape
    rows = groups * local_rows
    chunk = heads // chunks
    part = map_buf.shape[2]
    scale = width ** (-0.5)
    own = lax.axis_index("ctx")
    me = lax.axis_index("head")
    level = own // 2
    core = own % 2
    onward, back, side = own + 2, own - 2, own + 1 - 2 * core
    has_next = level < levels - 1
    has_map = has_next & (level >= 1)
    barrier = pltpu.get_barrier_semaphore()

    def greet(at):
        pl.semaphore_signal(barrier, inc=1, device_id={"ctx": at}, device_id_type=MESH)

    greet(side)

    @pl.when(has_next)
    def _():
        greet(onward)

    @pl.when(level >= 1)
    def _():
        greet(back)

    for p in range(1, groups):
        peer = (me + p) % groups
        pl.semaphore_signal(barrier, inc=1, device_id={"head": peer}, device_id_type=MESH)
    pl.semaphore_wait(
        barrier, groups + has_next.astype(jnp.int32) + (level >= 1).astype(jnp.int32)
    )

    def across(source, target, p, send, recv):
        return pltpu.make_async_remote_copy(
            src_ref=source,
            dst_ref=target,
            send_sem=send,
            recv_sem=recv,
            device_id={"head": (me + p) % groups},
            device_id_type=MESH,
        )

    def v_copy(p):
        to = value_buf.at[level, core, :, me]
        return across(v_ref.at[(me + p) % groups], to, p, v_send.at[p], v_arrive.at[p])

    def b_copy(p):
        to = logit_in.at[me]
        return across(logit_ref.at[(me + p) % groups], to, p, b_send.at[p], b_arrive.at[p])

    def x_copy(p, c):
        at = pl.ds(c * chunk, chunk)
        source = x_ref.at[(me + p) % groups, at]
        return across(source, x_in.at[me, at], p, x_send.at[p, c], x_arrive.at[p, c])

    def o_copy(p, h):
        source = out_buf.at[(me + p) % groups, h]
        return across(source, o_ref.at[me, h], p, o_send.at[p, h], o_arrive.at[p, h])

    kept = [
        pltpu.make_async_copy(v_ref.at[me], value_buf.at[level, core, :, me], keep.at[0]),
        pltpu.make_async_copy(logit_ref.at[me], logit_in.at[me], keep.at[1]),
        pltpu.make_async_copy(x_ref.at[me], x_in.at[me], keep.at[2]),
    ]
    for p in range(1, groups):
        b_copy(p).start()
        v_copy(p).start()
    for c in range(chunks):
        for p in range(1, groups):
            x_copy(p, c).start()
    for one_copy in kept:
        one_copy.start()
    for p in range(1, groups):
        b_copy(p).wait_recv()
        v_copy(p).wait_recv()
    for one_copy in kept:
        one_copy.wait()
    v_own = value_buf.at[level, core]

    def value_rows(at, c, h):
        if local_rows % 16 == 0:
            return value_buf[at, c, h].reshape(rows, width)
        pieces = [value_buf[at, c, h, s].astype(f32) for s in range(groups)]
        return jnp.concatenate(pieces, axis=0).astype(bf16)

    def slot(at, column, kind):
        if isinstance(kind, int) and kind < KEYS:
            return (value_buf, map_buf)[kind].at[at, column]
        return key_buf.at[at, column, pl.ds((kind - KEYS) * chunk, chunk)]

    def copy(source, at, kind, target, send):
        return pltpu.make_async_remote_copy(
            src_ref=source,
            dst_ref=slot(at, core, kind),
            send_sem=send.at[at, kind],
            recv_sem=arrive.at[at, core, kind],
            device_id={"ctx": target},
            device_id_type=MESH,
        )

    def send_next(source, at, kind):
        copy(source, at, kind, onward, send_on).start()

    def await_slot(at, column, kind):
        pltpu.make_async_remote_copy(
            src_ref=slot(at, column, kind),
            dst_ref=slot(at, column, kind),
            send_sem=send_side.at[at, kind],
            recv_sem=arrive.at[at, column, kind],
            device_id={"ctx": side},
            device_id_type=MESH,
        ).wait_recv()

    def relay(at, kind):
        await_slot(at, core, kind)

        @pl.when(has_next)
        def _():
            send_next(slot(at, core, kind), at, kind)

        copy(slot(at, core, kind), at, kind, side, send_side).start()

    @pl.when(has_next)
    def _():
        send_next(v_own, level, VALUES)

    @pl.when(core == 0)
    def _():
        copy(v_own, level, VALUES, side, send_side).start()

    at_row = lax.broadcasted_iota(jnp.int32, (local_rows, local_rows), 0)
    at_col = lax.broadcasted_iota(jnp.int32, (local_rows, local_rows), 1)

    def upright(row):
        return jnp.sum(jnp.where(at_row == at_col, row, 0.0), axis=1, keepdims=True)

    def local(h, carry):
        joined = lambda xs: jnp.concatenate(xs, axis=0)
        q0, k0, d0 = [
            joined([x_in[s, h, kind].astype(f32) for s in range(groups)]) for kind in range(3)
        ]
        v0 = value_rows(level, core, h)
        logit = joined([upright(logit_in[s, pl.ds(h, 1), :]) for s in range(groups)])
        m, l, a, q, k, moved = local_head(q0, k0, v0, d0, logit, frame)
        top[h] = m
        total[h] = l
        acc[h] = a
        query[h] = q
        key_wide[h] = k
        key_self[h] = k.astype(bf16)
        own_map[h] = moved
        return carry

    for c in range(chunks):
        for p in range(1, groups):
            x_copy(p, c).wait_recv()
        lax.fori_loop(c * chunk, (c + 1) * chunk, local, 0)

        @pl.when((core == 1) & has_next)
        def _():
            send_next(key_self.at[pl.ds(c * chunk, chunk)], level, KEYS + c)

        if c == 0:

            @pl.when(level >= 1)
            def _():
                relay(level - 1, VALUES)

        if c == min(2, chunks - 1):

            @pl.when(level >= 2)
            def _():
                relay(level - 2, VALUES)

    swap = pltpu.make_async_remote_copy(
        src_ref=own_map,
        dst_ref=side_map,
        send_sem=pair_send,
        recv_sem=pair_arrive,
        device_id={"ctx": side},
        device_id_type=MESH,
    )
    swap.start()

    @pl.when(core == 0)
    def _():
        for c in range(chunks):
            source = key_self.at[pl.ds(c * chunk, chunk)]
            copy(source, level, KEYS + c, side, send_side).start()

    swap.wait_recv()

    @pl.when((core == 0) & has_next)
    def _():
        def rebase(h, carry):
            key_buf[level, 0, h] = wide_nt(key_wide[h], side_map[h]).astype(bf16)
            return carry

        for c in range(chunks):
            lax.fori_loop(c * chunk, (c + 1) * chunk, rebase, 0)
            if c >= 1:
                send_next(slot(level, 0, KEYS + c - 1), level, KEYS + c - 1)
        send_next(slot(level, 0, KEYS + chunks - 1), level, KEYS + chunks - 1)

    @pl.when(has_map & (core == 0))
    def _():
        for i in range(part):
            map_buf[level, 0, i] = wide(side_map[i], own_map[i])

    @pl.when(has_map & (core == 1))
    def _():
        for i in range(part):
            map_buf[level, 1, i] = wide(own_map[part + i], side_map[part + i])

    @pl.when(has_map)
    def _():
        send_next(slot(level, core, MAPS), level, MAPS)

    def absorb(h, pieces):
        current = query[h].astype(bf16)
        scores = [mm_nt(current, key_buf[at, c, h]) * scale for at, c in pieces]
        new = top[h]
        for s in scores:
            new = jnp.maximum(new, jnp.max(s, axis=1, keepdims=True))
        factor = jnp.exp(top[h] - new)
        amount = total[h] * factor
        weighted = acc[h] * factor
        for s, (at, c) in zip(scores, pieces):
            w = jnp.exp(s - new)
            amount = amount + jnp.sum(w, axis=1, keepdims=True)
            weighted = weighted + mm(w.astype(bf16), value_rows(at, c, h))
        top[h] = new
        total[h] = amount
        acc[h] = weighted

    def finish(h):
        out = acc[h] / total[h]
        for s in range(groups):
            piece = out[s * local_rows : (s + 1) * local_rows].astype(bf16)
            out_buf[s, h] = piece

    def hand_back(h):
        for p in range(1, groups):
            o_copy(p, h).start()

    def close(h):
        finish(h)

        @pl.when(h >= 1)
        def _():
            hand_back(h - 1)

    @pl.when(core == 1)
    def _():
        await_slot(level, 0, VALUES)
        for c in range(chunks):
            await_slot(level, 0, KEYS + c)

        def near(h, carry):
            absorb(h, [(level, 0)])
            query[h] = wide(query[h], side_map[h])
            return carry

        lax.fori_loop(0, heads, near, 0)

    def far(i, carry):
        at = level - 1 - i

        @pl.when(i >= 2)
        def _():
            relay(at, VALUES)

        await_slot(at, 1 - core, VALUES)

        def some(c, inner):
            relay(at, KEYS + c)
            await_slot(at, 1 - core, KEYS + c)
            return lax.fori_loop(c * chunk, (c + 1) * chunk, one, inner)

        def one(h, inner):
            absorb(h, [(at, 1), (at, 0)])

            @pl.when(at == 0)
            def _():
                close(h)

            return inner

        lax.fori_loop(0, chunks, some, 0)

        @pl.when(at >= 1)
        def _():
            relay(at, MAPS)

        @pl.when(at >= 1)
        def _():
            await_slot(at, 1 - core, MAPS)

            def move(h, inner):
                query[h] = wide(query[h], map_buf[at, h // part, h % part])
                return inner

            lax.fori_loop(0, heads, move, 0)

        return carry

    lax.fori_loop(0, level, far, 0)

    @pl.when(level == 0)
    def _():
        def last(h, carry):
            close(h)
            return carry

        lax.fori_loop(0, heads, last, 0)

    o_ref[me] = out_buf[me]
    hand_back(heads - 1)

    def settle(at, kind, target, send):
        copy(slot(at, core, kind), at, kind, target, send).wait_send()

    def settle_side(at, carry):
        for c in range(chunks):
            settle(at, KEYS + c, side, send_side)
        settle(at, VALUES, side, send_side)

        @pl.when(at >= 1)
        def _():
            settle(at, MAPS, side, send_side)

        return carry

    def settle_next(at, carry):
        for c in range(chunks):
            settle(at, KEYS + c, onward, send_on)
        settle(at, VALUES, onward, send_on)

        @pl.when(at >= 1)
        def _():
            settle(at, MAPS, onward, send_on)

        return carry

    lax.fori_loop(0, level, settle_side, 0)

    @pl.when(core == 0)
    def _():
        for c in range(chunks):
            settle(level, KEYS + c, side, send_side)
        settle(level, VALUES, side, send_side)

    @pl.when(has_next)
    def _():
        lax.fori_loop(0, level + 1, settle_next, 0)

    swap.wait_send()
    for p in range(1, groups):
        b_copy(p).wait_send()
        v_copy(p).wait_send()
        for c in range(chunks):
            x_copy(p, c).wait_send()

        def handed(h, carry):
            o_copy(p, h).wait()
            return carry

        lax.fori_loop(0, heads, handed, 0)


def shards(queries, key_vectors, values, directions, beta_logit):
    groups = lax.axis_size("head")
    levels = lax.axis_size("ctx") // 2
    local_rows, head_total, width = queries.shape
    heads = head_total // groups
    rows = local_rows * groups

    def outgoing(x):
        return x.reshape(local_rows, groups, heads, width).transpose(1, 2, 0, 3)

    stacked = jnp.stack([outgoing(x) for x in (queries, key_vectors, directions)], axis=2)
    value_rows = outgoing(values)
    logit = beta_logit.reshape(local_rows, groups, heads).transpose(1, 2, 0).astype(f32)
    chunks = 4 if heads % 4 == 0 else heads
    part = heads // 2
    vmem = pl.BlockSpec(memory_space=pltpu.VMEM)
    out = pl.pallas_call(
        functools.partial(block_kernel, groups, levels, 2 * SUB, chunks),
        in_specs=[vmem] * 3,
        out_specs=vmem,
        out_shape=jax.ShapeDtypeStruct((groups, heads, local_rows, width), bf16),
        scratch_shapes=[
            pltpu.VMEM(stacked.shape, bf16),
            pltpu.VMEM(logit.shape, f32),
            pltpu.VMEM((groups, heads, local_rows, width), bf16),
            pltpu.VMEM((levels, 2, heads, rows, width), bf16),
            pltpu.VMEM((levels, 2, heads, groups, local_rows, width), bf16),
            pltpu.VMEM((levels, 2, part, width, width), f32),
            pltpu.VMEM((heads, rows, width), bf16),
            pltpu.VMEM((heads, rows, width), f32),
            pltpu.VMEM((heads, rows, width), f32),
            pltpu.VMEM((heads, rows, width), f32),
            pltpu.VMEM((heads, rows, 1), f32),
            pltpu.VMEM((heads, rows, 1), f32),
            pltpu.VMEM((heads, width, width), f32),
            pltpu.VMEM((heads, width, width), f32),
            pltpu.SemaphoreType.DMA((levels, KEYS + chunks)),
            pltpu.SemaphoreType.DMA((levels, KEYS + chunks)),
            pltpu.SemaphoreType.DMA((levels, 2, KEYS + chunks)),
            pltpu.SemaphoreType.DMA,
            pltpu.SemaphoreType.DMA,
            pltpu.SemaphoreType.DMA((groups, chunks)),
            pltpu.SemaphoreType.DMA((groups, chunks)),
            pltpu.SemaphoreType.DMA((groups,)),
            pltpu.SemaphoreType.DMA((groups,)),
            pltpu.SemaphoreType.DMA((groups,)),
            pltpu.SemaphoreType.DMA((groups,)),
            pltpu.SemaphoreType.DMA((groups, heads)),
            pltpu.SemaphoreType.DMA((groups, heads)),
            pltpu.SemaphoreType.DMA((3,)),
        ],
        compiler_params=pltpu.CompilerParams(collective_id=0, has_side_effects=True),
        name="block_chain",
    )(stacked, value_rows, logit)
    return out.transpose(2, 0, 1, 3).reshape(local_rows, head_total, width)


def solution(mesh):
    rows = P(("ctx", "head"), None, None)
    in_specs = (rows, rows, rows, rows, P(("ctx", "head"), None))
    return jax.shard_map(shards, mesh=mesh, in_specs=in_specs, out_specs=rows, check_vma=False)
```
